32 devices in a mesh: grp: 2 (over x), rows: 16 (over z, y, core).
Axes of the slice: x: 2, y: 2, z: 4, core: 2. Of those that a mesh axis runs over, the one named last changes fastest.
Arguments:
- histories: float32 [4096, 384], P(('grp', 'rows')), parts along dimension 0, may hold values from -6 to 6
- modal_map: float32 [4096, 8192], P(('grp', 'rows')), parts along dimension 0, may hold values from -0.1875 to 0.1875
- recovery: float32 [8192, 8192], P(('grp', 'rows')), parts along dimension 0, may hold values from -0.0625 to 0.0625
Outputs:
- responses: float32 [8192, 384], P(('grp', 'rows')), parts along dimension 0
- peak_response: float32 [4, 8192], P(None, ('grp', 'rows')), parts along dimension 1
- rms_response: float32 [4, 8192], P(None, ('grp', 'rows')), parts along dimension 1
The draws below stay inside these ranges and needn't reach their ends.
There are 2 independent parts, one for each index of `grp`. The reference program is written for one: setup_inputs(seed, part) draws one part's arguments, and reference() takes and returns one part's arrays. A program takes and returns all parts, laid end to end along the dimension named above; each array names one. Nothing has to cross between parts.
All inputs are finite; a program needn't handle non-finite values.
Results may differ from the reference program's by a relative error of at most 0.000071.
Values sent between devices are 32-bit elements; how exact they have to be, the bound alone decides.
A program may use at most 64 MiB of HBM per device.

```python
import jax
import jax.numpy as jnp
from jax import lax

MODES = 8192
COUPLED = 2048
CASES = 4
STEPS = 96
OUTPUTS = 4096
TIME = 384


def raised(drawn, stream_key, source, target, parts, factor):
    owner, partner = [(jnp.arange(drawn.shape[axis_at]) // (drawn.shape[axis_at] // parts)).reshape([-1 if axis == axis_at else 1 for axis in range(drawn.ndim)]) for axis_at in (source, target)]
    chosen = jax.random.permutation(stream_key, parts)[partner]
    strong = (owner == chosen) | (owner == (partner + parts // 2) % parts)
    return jnp.where(strong, factor * drawn, drawn)


def block_scale(rng, shape, split, smallest, high):
    factor_of = 1.0
    for dim, shards_of in split:
        draws = jax.random.uniform(jax.random.fold_in(jax.random.fold_in(rng, 6), dim), (shards_of,), jnp.float32, smallest / len(split), high / len(split))
        factor_of = factor_of * jnp.repeat(jnp.exp(draws), shape[dim] // shards_of).reshape((-1,) + (1,) * (len(shape) - 1 - dim))
    return factor_of


def bell_draw(stream_key, shape, spread, most, split=(), held_as=jnp.bfloat16):
    values = jax.random.normal(stream_key, shape, jnp.float32) * spread
    if len(split) > 0:
        values = block_scale(stream_key, shape, split, -0.22, 0.18) * values
    return jnp.clip(values, min=-most, max=most).astype(held_as)


def gaussian_with(own_key, extent, deviation, bound, shards, heavy, dtype=jnp.bfloat16):
    drawn = deviation * jax.random.normal(own_key, extent, jnp.float32)
    if shards:
        drawn = drawn * block_scale(own_key, extent, shards, -0.22, 0.18)
    return jnp.clip(raised(drawn, jax.random.fold_in(own_key, 3), *heavy), -bound, bound).astype(dtype)


def setup_inputs(seed: int = 0, part: int = 0) -> dict:
    streams_of = jax.random.split(jax.random.key(seed), 4)
    part_keys = jax.random.split(jax.random.fold_in(streams_of[3], part), 4)
    return {
        "histories": bell_draw(part_keys[0], (COUPLED, TIME), 1.0, 6.0, ((0, 16),), jnp.float32),
        "modal_map": gaussian_with(part_keys[1], (COUPLED, MODES), COUPLED ** -0.5, 0.1875, ((0, 16),), (0, 1, 16, 2.0), jnp.float32),
        "recovery": bell_draw(part_keys[2], (OUTPUTS, MODES), MODES ** -0.5, 0.0625, ((0, 16),), jnp.float32),
    }


epsilon = 1e-06

def reference(histories, modal_map, recovery):
    modal_rows = lax.dot_general(modal_map, histories, (((0,), (0,)), ((), ())), precision=lax.Precision.HIGHEST, preferred_element_type=jnp.float32)
    responses = jnp.dot(recovery, modal_rows, precision=lax.Precision.HIGHEST, preferred_element_type=jnp.float32)
    by_case = responses.reshape(responses.shape[0], CASES, STEPS)
    peak_response = lax.optimization_barrier(jnp.max(jnp.abs(by_case), axis=2)).T
    rms_response = jnp.sqrt(lax.optimization_barrier(jnp.mean(by_case * by_case, axis=2)) + epsilon).T
    return (responses, peak_response, rms_response)
```

```python
import functools

import jax
import jax.numpy as jnp
from jax import lax
from jax.experimental import pallas as pl
from jax.experimental.pallas import tpu as pltpu
from jax.sharding import PartitionSpec as P

CASES = 4
SUBS = 2
epsilon = 1e-06
MESH = pl.DeviceIdType.MESH


def split(x):
    high = x.astype(jnp.bfloat16)
    return high, (x - high.astype(jnp.float32)).astype(jnp.bfloat16)


def dot3(a, b, dims):
    mul = functools.partial(
        lax.dot_general, dimension_numbers=(dims, ((), ())), preferred_element_type=jnp.float32
    )
    return mul(a[0], b[0]) + (mul(a[0], b[1]) + mul(a[1], b[0]))


def ring_position(chips, chip):
    if chips == 8:
        z, y = chip // 2, chip % 2
        return y * (chips - 1 - 2 * z) + z
    return chip


def chip_at(chips, position):
    if chips == 8:
        y = position // 4
        return (y * (chips - 1 - 2 * position) + position) * 2 + y
    return position


def kernel(
    chips, ways, h_ref, m_ref, r_ref, out_ref, peak_ref, rms_ref,
    h_other, hist_hi, hist_lo, m_buf, r_buf, part, landed, rows, acc, acc_other,
    local_sem, pair_send, pair_recv, m_send, m_recv, rs_send, rs_recv, ag_send, ag_recv,
):
    me = lax.axis_index("rows")
    core = me % 2
    partner = me + 1 - 2 * core
    pos = ring_position(chips, me // 2)
    after = chip_at(chips, (pos + 1) % chips) * 2 + core
    before = chip_at(chips, (pos + chips - 1) % chips) * 2 + core
    targets = (after, before)
    signs = (1, -1)

    modes, outs = h_ref.shape[0], r_ref.shape[0]
    half = m_ref.shape[1] // 2
    block = half // chips
    unit = block // ways
    piece = unit // SUBS

    def at(p):
        return (p + 2 * chips) % chips

    def cols(base, b, d):
        return pl.ds(pl.multiple_of(base + b * block + d * unit, 128), unit)

    def remote(src, dst, send, recv, to):
        return pltpu.make_async_remote_copy(
            src_ref=src, dst_ref=dst, send_sem=send, recv_sem=recv,
            device_id={"rows": to}, device_id_type=MESH,
        )

    def sum_block(k, d):
        return at(pos - signs[d] * (k + 1))

    def m_copy(k, d):
        b = sum_block(k, d)
        return remote(
            m_ref.at[:, cols((1 - core) * half, b, d)],
            m_buf.at[pl.ds(modes, modes), cols(0, b, d)],
            m_send.at[d, k], m_recv.at[d, k], partner,
        )

    def rs_copy(k, d, j):
        view = (d, k, pl.ds(j * piece, piece))
        return remote(part.at[view], landed.at[view], rs_send.at[d, k, j], rs_recv.at[d, k, j], targets[d])

    def ag_copy(s, d, j, arrives=False):
        b = at(pos - signs[d] * (s + 1 if arrives else s))
        view = (b, d, pl.ds(j * piece, piece))
        return remote(rows.at[view], rows.at[view], ag_send.at[d, s, j], ag_recv.at[d, s, j], targets[d])

    own_m = pltpu.make_async_copy(
        m_ref.at[:, pl.ds(pl.multiple_of(core * half, 128), half)],
        m_buf.at[pl.ds(0, modes)], local_sem.at[0],
    )
    own_r = pltpu.make_async_copy(
        r_ref.at[:, pl.ds(pl.multiple_of(core * half, 128), half)],
        r_buf.at[pl.ds(0, outs)], local_sem.at[1],
    )
    h_copy = remote(h_ref, h_other, pair_send.at[0], pair_recv.at[0], partner)
    r_copy = remote(
        r_ref.at[:, pl.ds(pl.multiple_of((1 - core) * half, 128), half)],
        r_buf.at[pl.ds(outs, outs)], pair_send.at[1], pair_recv.at[1], partner,
    )
    acc_copy = remote(acc.at[pl.ds(outs, outs)], acc_other, pair_send.at[2], pair_recv.at[2], partner)

    own_m.start()
    own_r.start()
    barrier = pltpu.get_barrier_semaphore()
    for other in (after, before, partner):
        pl.semaphore_signal(barrier, inc=1, device_id={"rows": other}, device_id_type=MESH)
    pl.semaphore_wait(barrier, 3)

    h_copy.start()

    @pl.loop(0, chips)
    def _(k):
        for d in range(ways):
            m_copy(k, d).start()

    r_copy.start()
    own_m.wait()
    h_copy.wait_recv()
    for src, base in ((h_ref, 0), (h_other, modes)):
        hist_hi[pl.ds(base, modes)], hist_lo[pl.ds(base, modes)] = split(src[...])

    def partial_rows(k, d):
        m_copy(k, d).wait_recv()
        shapes = split(m_buf[:, cols(0, sum_block(k, d), d)])
        return dot3(shapes, (hist_hi[...], hist_lo[...]), ((0,), (0,)))

    for d in range(ways):
        part[d, 0] = partial_rows(0, d)
        for j in range(SUBS):
            rs_copy(0, d, j).start()

    @pl.loop(1, chips - 1)
    def _(k):
        for d in range(ways):
            part[d, k] = partial_rows(k, d)
        for j in range(SUBS):
            for d in range(ways):
                rs_copy(k - 1, d, j).wait_recv()
                view = (d, k, pl.ds(j * piece, piece))
                part[view] = part[view] + landed[d, k - 1, pl.ds(j * piece, piece)]
                rs_copy(k, d, j).start()

    last = chips - 1
    for d in range(ways):
        rows[pos, d] = partial_rows(last, d)
    for j in range(SUBS):
        for d in range(ways):
            rs_copy(last - 1, d, j).wait_recv()
            view = (pos, d, pl.ds(j * piece, piece))
            rows[view] = rows[view] + landed[d, last - 1, pl.ds(j * piece, piece)]
            ag_copy(0, d, j).start()

    own_r.wait()
    r_copy.wait_recv()

    def recovered(b, d):
        return dot3(split(r_buf[:, cols(0, b, d)]), split(rows[b, d]), ((1,), (0,)))

    acc[...] = recovered(pos, 0)
    for d in range(1, ways):
        acc[...] += recovered(pos, d)

    @pl.loop(0, chips - 2)
    def _(s):
        for j in range(SUBS):
            for d in range(ways):
                ag_copy(s, d, j, arrives=True).wait_recv()
                ag_copy(s + 1, d, j).start()
        for d in range(ways):
            acc[...] += recovered(at(pos - signs[d] * (s + 1)), d)

    for d in range(ways):
        for j in range(SUBS):
            ag_copy(chips - 2, d, j, arrives=True).wait_recv()
        acc[...] += recovered(at(pos - signs[d] * (chips - 1)), d)

    acc_copy.start()

    h_copy.wait_send()
    r_copy.wait_send()

    @pl.loop(0, chips)
    def _(k):
        for d in range(ways):
            m_copy(k, d).wait_send()

    @pl.loop(0, chips - 1)
    def _(k):
        for d in range(ways):
            for j in range(SUBS):
                rs_copy(k, d, j).wait_send()
                ag_copy(k, d, j).wait_send()

    acc_copy.wait()
    responses = acc[pl.ds(0, outs)] + acc_other[...]
    out_ref[...] = responses
    by_time = responses.T
    steps = by_time.shape[0] // CASES
    for k in range(CASES):
        case = by_time[k * steps : (k + 1) * steps]
        peak_ref[k : k + 1] = jnp.max(jnp.abs(case), axis=0, keepdims=True)
        mean = jnp.sum(case * case, axis=0, keepdims=True) / steps
        rms_ref[k : k + 1] = jnp.sqrt(mean + epsilon)


def shards(size, histories, modal_map, recovery):
    chips = size // 2
    modes, time_cols = histories.shape
    outs, dofs = recovery.shape
    half = dofs // 2
    block = half // chips
    ways = 2 if block % 256 == 0 else 1
    unit = block // ways
    f32, dma = jnp.float32, pltpu.SemaphoreType.DMA
    vmem, anywhere = pl.BlockSpec(memory_space=pltpu.VMEM), pl.BlockSpec(memory_space=pl.ANY)
    return pl.pallas_call(
        functools.partial(kernel, chips, ways),
        out_shape=(
            jax.ShapeDtypeStruct((outs, time_cols), f32),
            jax.ShapeDtypeStruct((CASES, outs), f32),
            jax.ShapeDtypeStruct((CASES, outs), f32),
        ),
        in_specs=[vmem, anywhere, anywhere],
        out_specs=(vmem, vmem, vmem),
        scratch_shapes=[
            pltpu.VMEM((modes, time_cols), f32),
            pltpu.VMEM((2 * modes, time_cols), jnp.bfloat16),
            pltpu.VMEM((2 * modes, time_cols), jnp.bfloat16),
            pltpu.VMEM((2 * modes, half), f32),
            pltpu.VMEM((2 * outs, half), f32),
            pltpu.VMEM((ways, chips - 1, unit, time_cols), f32),
            pltpu.VMEM((ways, chips - 1, unit, time_cols), f32),
            pltpu.VMEM((chips, ways, unit, time_cols), f32),
            pltpu.VMEM((2 * outs, time_cols), f32),
            pltpu.VMEM((outs, time_cols), f32),
            dma((2,)),
            dma((3,)),
            dma((3,)),
            dma((ways, chips)),
            dma((ways, chips)),
            dma((ways, chips - 1, SUBS)),
            dma((ways, chips - 1, SUBS)),
            dma((ways, chips - 1, SUBS)),
            dma((ways, chips - 1, SUBS)),
        ],
        compiler_params=pltpu.CompilerParams(
            collective_id=0, has_side_effects=True, vmem_limit_bytes=50 * 2**20
        ),
    )(histories, modal_map, recovery)


def solution(mesh):
    return jax.shard_map(
        functools.partial(shards, mesh.shape["rows"]),
        mesh=mesh,
        in_specs=(P(("grp", "rows"), None), P(("grp", "rows"), None), P(("grp", "rows"), None)),
        out_specs=(P(("grp", "rows"), None), P(None, ("grp", "rows")), P(None, ("grp", "rows"))),
        check_vma=False,
    )
```

```python
import functools

import jax
import jax.numpy as jnp
from jax import lax
from jax.experimental import pallas as pl
from jax.experimental.pallas import tpu as pltpu
from jax.sharding import PartitionSpec as P

CASES = 4
SUBS = 2
epsilon = 1e-06
MESH = pl.DeviceIdType.MESH


def split(x):
    high = x.astype(jnp.bfloat16)
    return high, (x - high.astype(jnp.float32)).astype(jnp.bfloat16)


def dot3(a, b, dims):
    mul = functools.partial(
        lax.dot_general, dimension_numbers=(dims, ((), ())), preferred_element_type=jnp.float32
    )
    return mul(a[0], b[0]) + (mul(a[0], b[1]) + mul(a[1], b[0]))


def ring_position(chips, chip):
    if chips == 8:
        z, y = chip // 2, chip % 2
        return y * (chips - 1 - 2 * z) + z
    return chip


def chip_at(chips, position):
    if chips == 8:
        y = position // 4
        return (y * (chips - 1 - 2 * position) + position) * 2 + y
    return position


def kernel(
    chips, ways, h_ref, m_ref, r_ref, out_ref,
    hist, hist_hi, hist_lo, m_buf, r_buf, part, landed, rows, acc, acc_other,
    local_sem, pair_send, pair_recv, m_local, m_send, m_recv, rs_send, rs_recv, ag_send, ag_recv,
):
    me = lax.axis_index("rows")
    core = me % 2
    partner = me + 1 - 2 * core
    pos = ring_position(chips, me // 2)
    after = chip_at(chips, (pos + 1) % chips) * 2 + core
    before = chip_at(chips, (pos + chips - 1) % chips) * 2 + core
    targets = (after, before)
    signs = (1, -1)

    modes, outs = h_ref.shape[0], r_ref.shape[0]
    half = m_ref.shape[1] // 2
    block = half // chips
    unit = block // ways
    piece = unit // SUBS
    cuts = SUBS if piece % 128 == 0 else 1
    width = unit // cuts

    def at(p):
        return (p + 2 * chips) % chips

    def cols(base, b, d, start=0, size=unit):
        return pl.ds(pl.multiple_of(base + b * block + d * unit + start, 128), size)

    def remote(src, dst, send, recv, to):
        return pltpu.make_async_remote_copy(
            src_ref=src, dst_ref=dst, send_sem=send, recv_sem=recv,
            device_id={"rows": to}, device_id_type=MESH,
        )

    def sum_block(k, d):
        return at(pos - signs[d] * (k + 1))

    def m_copy(k, d):
        b = sum_block(k, d)
        return remote(
            m_ref.at[:, cols((1 - core) * half, b, d)],
            m_buf.at[pl.ds(modes, modes), cols(0, b, d)],
            m_send.at[d, k], m_recv.at[d, k], partner,
        )

    def own_m(k, d):
        b = sum_block(k, d)
        return pltpu.make_async_copy(
            m_ref.at[:, cols(core * half, b, d)],
            m_buf.at[pl.ds(0, modes), cols(0, b, d)], m_local.at[d, k],
        )

    def rs_copy(k, d, j):
        view = (d, k, pl.ds(j * piece, piece))
        return remote(part.at[view], landed.at[view], rs_send.at[d, k, j], rs_recv.at[d, k, j], targets[d])

    def ag_copy(s, d, j, arrives=False):
        b = at(pos - signs[d] * (s + 1 if arrives else s))
        view = (b, d, pl.ds(j * piece, piece))
        return remote(rows.at[view], rows.at[view], ag_send.at[d, s, j], ag_recv.at[d, s, j], targets[d])

    own_h = pltpu.make_async_copy(h_ref, hist.at[pl.ds(0, modes)], local_sem.at[0])
    own_r = pltpu.make_async_copy(
        r_ref.at[:, pl.ds(pl.multiple_of(core * half, 128), half)],
        r_buf.at[pl.ds(0, outs)], local_sem.at[1],
    )
    h_copy = remote(h_ref, hist.at[pl.ds(modes, modes)], pair_send.at[0], pair_recv.at[0], partner)
    r_copy = remote(
        r_ref.at[:, pl.ds(pl.multiple_of((1 - core) * half, 128), half)],
        r_buf.at[pl.ds(outs, outs)], pair_send.at[1], pair_recv.at[1], partner,
    )
    acc_copy = remote(acc.at[pl.ds(outs, outs)], acc_other, pair_send.at[2], pair_recv.at[2], partner)

    own_h.start()
    for d in range(ways):
        own_m(0, d).start()
    barrier = pltpu.get_barrier_semaphore()
    for other in (after, before, partner):
        pl.semaphore_signal(barrier, inc=1, device_id={"rows": other}, device_id_type=MESH)
    pl.semaphore_wait(barrier, 3)

    h_copy.start()
    for d in range(ways):
        m_copy(0, d).start()

    @pl.loop(1, chips)
    def _(k):
        for d in range(ways):
            own_m(k, d).start()
            m_copy(k, d).start()

    own_h.wait()
    hist_hi[pl.ds(0, modes)], hist_lo[pl.ds(0, modes)] = split(hist[pl.ds(0, modes)])
    h_copy.wait_recv()
    hist_hi[pl.ds(modes, modes)], hist_lo[pl.ds(modes, modes)] = split(hist[pl.ds(modes, modes)])

    def shapes_here(k, d):
        own_m(k, d).wait()
        m_copy(k, d).wait_recv()

    def partial_rows(k, d, start=0, size=unit):
        shapes = split(m_buf[:, cols(0, sum_block(k, d), d, start, size)])
        return dot3(shapes, (hist_hi[...], hist_lo[...]), ((0,), (0,)))

    for cut in range(cuts):
        for d in range(ways):
            if cut == 0:
                shapes_here(0, d)
            start = cut * width
            part[d, 0, pl.ds(start, width)] = partial_rows(0, d, start, width)
            for j in range(cut * SUBS // cuts, (cut + 1) * SUBS // cuts):
                rs_copy(0, d, j).start()

    own_r.start()
    r_copy.start()

    @pl.loop(1, chips - 1)
    def _(k):
        for d in range(ways):
            shapes_here(k, d)
            part[d, k] = partial_rows(k, d)
        for j in range(SUBS):
            for d in range(ways):
                rs_copy(k - 1, d, j).wait_recv()
                view = (d, k, pl.ds(j * piece, piece))
                part[view] = part[view] + landed[d, k - 1, pl.ds(j * piece, piece)]
                rs_copy(k, d, j).start()

    last = chips - 1
    for d in range(ways):
        shapes_here(last, d)
        rows[pos, d] = partial_rows(last, d)
    for j in range(SUBS):
        for d in range(ways):
            rs_copy(last - 1, d, j).wait_recv()
            view = (pos, d, pl.ds(j * piece, piece))
            rows[view] = rows[view] + landed[d, last - 1, pl.ds(j * piece, piece)]
            ag_copy(0, d, j).start()

    own_r.wait()
    r_copy.wait_recv()

    def recovered(b, d):
        return dot3(split(r_buf[:, cols(0, b, d)]), split(rows[b, d]), ((1,), (0,)))

    acc[...] = recovered(pos, 0)
    for d in range(1, ways):
        acc[...] += recovered(pos, d)

    @pl.loop(0, chips - 2)
    def _(s):
        for j in range(SUBS):
            for d in range(ways):
                ag_copy(s, d, j, arrives=True).wait_recv()
                ag_copy(s + 1, d, j).start()
        for d in range(ways):
            acc[...] += recovered(at(pos - signs[d] * (s + 1)), d)

    for cut in range(cuts):
        for d in range(ways):
            for j in range(cut * SUBS // cuts, (cut + 1) * SUBS // cuts):
                ag_copy(chips - 2, d, j, arrives=True).wait_recv()
            b, start = at(pos - signs[d] * (chips - 1)), cut * width
            weights = split(r_buf[:, cols(0, b, d, start, width)])
            finished = split(rows[b, d, pl.ds(start, width)])
            final = cut == cuts - 1 and d == ways - 1
            for base in (outs, 0):
                own = tuple(w[base : base + outs] for w in weights)
                acc[pl.ds(base, outs)] += dot3(own, finished, ((1,), (0,)))
                if final and base:
                    acc_copy.start()

    h_copy.wait_send()
    r_copy.wait_send()

    @pl.loop(0, chips)
    def _(k):
        for d in range(ways):
            m_copy(k, d).wait_send()

    @pl.loop(0, chips - 1)
    def _(k):
        for d in range(ways):
            for j in range(SUBS):
                rs_copy(k, d, j).wait_send()
                ag_copy(k, d, j).wait_send()

    acc_copy.wait()
    out_ref[...] = acc[pl.ds(0, outs)] + acc_other[...]


def statistics(found_ref, out_ref, peak_ref, rms_ref):
    responses = found_ref[...]
    out_ref[...] = responses
    by_time = responses.T
    steps = by_time.shape[0] // CASES
    for k in range(CASES):
        case = by_time[k * steps : (k + 1) * steps]
        peak_ref[k : k + 1] = jnp.max(jnp.abs(case), axis=0, keepdims=True)
        mean = jnp.sum(case * case, axis=0, keepdims=True) / steps
        rms_ref[k : k + 1] = jnp.sqrt(mean + epsilon)


def shards(size, histories, modal_map, recovery):
    chips = size // 2
    modes, time_cols = histories.shape
    outs, dofs = recovery.shape
    half = dofs // 2
    block = half // chips
    ways = 2 if block % 256 == 0 else 1
    unit = block // ways
    f32, dma = jnp.float32, pltpu.SemaphoreType.DMA
    vmem, anywhere = pl.BlockSpec(memory_space=pltpu.VMEM), pl.BlockSpec(memory_space=pltpu.HBM)
    found = pl.pallas_call(
        functools.partial(kernel, chips, ways),
        out_shape=jax.ShapeDtypeStruct((outs, time_cols), f32),
        in_specs=[anywhere, anywhere, anywhere],
        out_specs=vmem,
        scratch_shapes=[
            pltpu.VMEM((2 * modes, time_cols), f32),
            pltpu.VMEM((2 * modes, time_cols), jnp.bfloat16),
            pltpu.VMEM((2 * modes, time_cols), jnp.bfloat16),
            pltpu.VMEM((2 * modes, half), f32),
            pltpu.VMEM((2 * outs, half), f32),
            pltpu.VMEM((ways, chips - 1, unit, time_cols), f32),
            pltpu.VMEM((ways, chips - 1, unit, time_cols), f32),
            pltpu.VMEM((chips, ways, unit, time_cols), f32),
            pltpu.VMEM((2 * outs, time_cols), f32),
            pltpu.VMEM((outs, time_cols), f32),
            dma((2,)),
            dma((3,)),
            dma((3,)),
            dma((ways, chips)),
            dma((ways, chips)),
            dma((ways, chips)),
            dma((ways, chips - 1, SUBS)),
            dma((ways, chips - 1, SUBS)),
            dma((ways, chips - 1, SUBS)),
            dma((ways, chips - 1, SUBS)),
        ],
        compiler_params=pltpu.CompilerParams(
            collective_id=0, has_side_effects=True, vmem_limit_bytes=50 * 2**20
        ),
    )(histories, modal_map, recovery)
    return pl.pallas_call(
        statistics,
        out_shape=(
            jax.ShapeDtypeStruct((outs, time_cols), f32),
            jax.ShapeDtypeStruct((CASES, outs), f32),
            jax.ShapeDtypeStruct((CASES, outs), f32),
        ),
        in_specs=[vmem], compiler_params=pltpu.CompilerParams(vmem_limit_bytes=8 * 2**20),
        out_specs=(vmem, vmem, vmem),
    )(found)


def solution(mesh):
    return jax.shard_map(
        functools.partial(shards, mesh.shape["rows"]),
        mesh=mesh,
        in_specs=(P(("grp", "rows"), None), P(("grp", "rows"), None), P(("grp", "rows"), None)),
        out_specs=(P(("grp", "rows"), None), P(None, ("grp", "rows")), P(None, ("grp", "rows"))),
        check_vma=False,
    )
```
